32 devices in a mesh: ctx: 8 (over y, x, core), fsdp: 4 (over z).
Axes of the slice: x: 2, y: 2, z: 4, core: 2. Of those that a mesh axis runs over, the one named last changes fastest.
Arguments:
- block_input: bfloat16 [4096, 768], P(('ctx', 'fsdp')), may hold values from -6 to 6
- positions: int32 [4096], replicated, may hold values from 0 to 4095, as said below
- norm1_gain: bfloat16 [768], P('fsdp'), may hold values from 0.5 to 1.5
- norm1_bias: bfloat16 [768], P('fsdp'), may hold values from -3 to 3
- qkv_weight: bfloat16 [768, 2304], P('fsdp'), may hold values from -0.21875 to 0.21875
- query_bias: bfloat16 [768], P('fsdp'), may hold values from -3 to 3
- value_bias: bfloat16 [768], P('fsdp'), may hold values from -3 to 3
- proj_weight: bfloat16 [768, 768], P('fsdp'), may hold values from -1.75 to 1.75
- proj_bias: bfloat16 [768], P('fsdp'), may hold values from -3 to 3
- norm2_gain: bfloat16 [768], P('fsdp'), may hold values from 0.5 to 1.5
- norm2_bias: bfloat16 [768], P('fsdp'), may hold values from -3 to 3
- fc_weight: bfloat16 [768, 3072], P('fsdp'), may hold values from -0.21875 to 0.21875
- fc_bias: bfloat16 [3072], P('fsdp'), may hold values from -3 to 3
- out_weight: bfloat16 [3072, 768], P('fsdp'), may hold values from -0.109375 to 0.109375
- out_bias: bfloat16 [768], P('fsdp'), may hold values from -3 to 3
- cotangent: bfloat16 [4096, 768], P(('ctx', 'fsdp')), may hold values from -6 to 6
Outputs:
- block_output: float32 [4096, 768], P(('ctx', 'fsdp'))
- input_grad: float32 [4096, 768], P(('ctx', 'fsdp'))
- norm1_gain_grad: float32 [768], P('fsdp')
- norm1_bias_grad: float32 [768], P('fsdp')
- qkv_weight_grad: float32 [768, 2304], P('fsdp')
- query_bias_grad: float32 [768], P('fsdp')
- value_bias_grad: float32 [768], P('fsdp')
- proj_weight_grad: float32 [768, 768], P('fsdp')
- proj_bias_grad: float32 [768], P('fsdp')
- norm2_gain_grad: float32 [768], P('fsdp')
- norm2_bias_grad: float32 [768], P('fsdp')
- fc_weight_grad: float32 [768, 3072], P('fsdp')
- fc_bias_grad: float32 [3072], P('fsdp')
- out_weight_grad: float32 [3072, 768], P('fsdp')
- out_bias_grad: float32 [768], P('fsdp')
The draws below stay inside these ranges and needn't reach their ends.
Inputs may be any that keep to these rules, and one draw needn't show every extreme that they name: positions is a permutation of 0 to 4095. For every g, the entries 2 * 256 * g to 2 * 256 * (g + 1) - 1 hold the 256 positions of a sequence block b_g in increasing order, then those of block 15 - b_g in increasing order; the b_g over all g are the numbers 0 to 7 in an order drawn from the seed.
All inputs are finite; a program needn't handle non-finite values.
Results may differ from the reference program's by a relative error of at most 0.03.
Values may be sent and summed in bfloat16 or wider, within the bound.
A program may use at most 128 MiB of HBM per device.

```python
import math
import jax
import jax.numpy as jnp
from jax import lax

D = 768
HEADS = 12
HEAD = 64
FF = 3072
BLOCK = 256
LENGTH = 4096


def draw_positions(key, part):
    group_count = LENGTH // (2 * BLOCK)
    lower_blocks = jax.random.permutation(jax.random.fold_in(key, 3), group_count).astype(jnp.int32)
    offsets = jnp.arange(BLOCK, dtype=jnp.int32)
    first_block = lower_blocks[:, None] * BLOCK + offsets[None, :]
    mirror_block = (2 * group_count - 1 - lower_blocks)[:, None] * BLOCK + offsets[None, :]
    ordered = jnp.concatenate([first_block, mirror_block], axis=1)
    return ordered.reshape(LENGTH).astype(jnp.int32)


def block_levels(key, extent, split, least, high):
    loudness = 1.0
    for position, shards_of in split:
        draws = jax.random.uniform(jax.random.fold_in(jax.random.fold_in(key, 6), position), (shards_of,), jnp.float32, least / len(split), high / len(split))
        loudness = loudness * jnp.repeat(jnp.exp(draws), extent[position] // shards_of).reshape((-1,) + (1,) * (len(extent) - 1 - position))
    return loudness


def normal_values(own_key, shape, scale, reach, cuts=(), kind=jnp.bfloat16):
    entries = jax.random.normal(own_key, shape, jnp.float32) * scale
    if len(cuts) > 0:
        entries = block_levels(own_key, shape, cuts, -0.22, 0.18) * entries
    return jnp.clip(entries, min=-reach, max=reach).astype(kind)


def setup_inputs(seed: int = 0) -> dict:
    splits = jax.random.split(jax.random.key(seed), 17)
    block_input = normal_values(splits[0], (LENGTH, D), 1.0, 6.0, ((0, 32),))
    positions = draw_positions(jax.random.fold_in(splits[16], 71), 0)
    norm1_gain = jnp.clip(1.0 + 0.1 * jax.random.normal(splits[2], (D,), jnp.float32), 0.5, 1.5).astype(jnp.bfloat16)
    norm1_bias = normal_values(splits[3], (D,), 0.5, 3.0, ((0, 4),))
    qkv_weight = normal_values(splits[4], (D, 3 * D), D ** -0.5, 0.21875, ((0, 4),))
    query_bias = normal_values(splits[5], (D,), 0.5, 3.0, ((0, 4),))
    value_bias = normal_values(splits[6], (D,), 0.5, 3.0, ((0, 4),))
    proj_weight = normal_values(splits[7], (D, D), (D // 64) ** -0.5, 1.75, ((0, 4),))
    proj_bias = normal_values(splits[8], (D,), 0.5, 3.0, ((0, 4),))
    norm2_gain = jnp.clip(1.0 + 0.1 * jax.random.normal(splits[9], (D,), jnp.float32), 0.5, 1.5).astype(jnp.bfloat16)
    norm2_bias = normal_values(splits[10], (D,), 0.5, 3.0, ((0, 4),))
    fc_weight = normal_values(splits[11], (D, FF), D ** -0.5, 0.21875, ((0, 4),))
    fc_bias = normal_values(splits[12], (FF,), 0.5, 3.0, ((0, 4),))
    out_weight = normal_values(splits[13], (FF, D), FF ** -0.5, 0.109375, ((0, 4),))
    out_bias = normal_values(splits[14], (D,), 0.5, 3.0, ((0, 4),))
    cotangent = normal_values(splits[15], (LENGTH, D), 1.0, 6.0, ((0, 32),))
    return {"block_input": block_input, "positions": positions, "norm1_gain": norm1_gain, "norm1_bias": norm1_bias, "qkv_weight": qkv_weight, "query_bias": query_bias, "value_bias": value_bias, "proj_weight": proj_weight, "proj_bias": proj_bias, "norm2_gain": norm2_gain, "norm2_bias": norm2_bias, "fc_weight": fc_weight, "fc_bias": fc_bias, "out_weight": out_weight, "out_bias": out_bias, "cotangent": cotangent}


EPSILON = 1e-05
NEG_FILL = -1e+30
GELU_C = 0.7978845608028654
GELU_K = 0.044715

def layer_norm(values_in, gain, shift):
    row_mean = lax.optimization_barrier(jnp.mean(values_in, axis=-1, keepdims=True))
    centered = values_in - row_mean
    variance = lax.optimization_barrier(jnp.mean(centered * centered, axis=-1, keepdims=True))
    inv_std = lax.rsqrt(variance + EPSILON)
    normed = centered * inv_std
    return (normed * gain.astype(jnp.float32) + shift.astype(jnp.float32), normed, inv_std)

def norm_backward(grad_norm, gain, normed, inv_std):
    scaled = grad_norm * gain.astype(jnp.float32)
    scaled_mean = lax.optimization_barrier(jnp.mean(scaled, axis=-1, keepdims=True))
    cross_mean = lax.optimization_barrier(jnp.mean(scaled * normed, axis=-1, keepdims=True))
    return inv_std * (scaled - scaled_mean - normed * cross_mean)

def gelu_forward(pre_act):
    cubed = pre_act * pre_act * pre_act
    return 0.5 * pre_act * (1.0 + jnp.tanh(GELU_C * (pre_act + GELU_K * cubed)))

def gelu_slope(pre_act):
    cubed = pre_act * pre_act * pre_act
    tanh_value = jnp.tanh(GELU_C * (pre_act + GELU_K * cubed))
    return 0.5 * (1.0 + tanh_value) + 0.5 * pre_act * (1.0 - tanh_value * tanh_value) * GELU_C * (1.0 + 3.0 * GELU_K * pre_act * pre_act)

def heads_of(matrix):
    return matrix.astype(jnp.float32).reshape(matrix.shape[0], HEADS, HEAD)

def tile_scores(query_block, query_pos, key_block, key_pos):
    scores = jnp.einsum('rhd,khd->hrk', heads_of(query_block), heads_of(key_block)) * HEAD ** (-0.5)
    allowed = (key_pos[None, :] <= query_pos[:, None])[None]
    return (jnp.where(allowed, scores, NEG_FILL), allowed)

def blocked(array_in, block_span):
    return array_in.reshape((array_in.shape[0] // block_span, block_span) + array_in.shape[1:])

def attention_forward(query, keys, values, positions):
    block_span = math.gcd(LENGTH, 2048)
    query_blocks = blocked(query, block_span)
    key_blocks = blocked(keys, block_span)
    value_blocks = blocked(values, block_span)
    pos_blocks = blocked(positions, block_span)

    def per_query(block_args):
        query_block, query_pos = block_args

        def max_step(carried, key_args):
            run_max, row_total = carried
            key_block, key_pos = key_args
            scores, allowed = tile_scores(query_block, query_pos, key_block, key_pos)
            new_max = jnp.maximum(run_max, lax.optimization_barrier(jnp.max(scores, axis=-1)))
            weights = jnp.where(allowed, jnp.exp(scores - new_max[..., None]), 0.0)
            row_total = row_total * jnp.exp(run_max - new_max) + lax.optimization_barrier(jnp.sum(weights, axis=-1))
            return ((new_max, row_total), None)
        initial = (jnp.full((HEADS, block_span), NEG_FILL, jnp.float32), jnp.zeros((HEADS, block_span), jnp.float32))
        stats, unused = lax.scan(max_step, initial, (key_blocks, pos_blocks))
        row_lse = stats[0] + jnp.log(stats[1])

        def out_step(weighted, key_args):
            key_block, value_block, key_pos = key_args
            scores, allowed = tile_scores(query_block, query_pos, key_block, key_pos)
            probs = jnp.where(allowed, jnp.exp(scores - row_lse[..., None]), 0.0)
            return (weighted + jnp.einsum('hrk,khd->rhd', probs, heads_of(value_block), precision=lax.Precision.HIGHEST), None)
        weighted, unused = lax.scan(out_step, jnp.zeros((block_span, HEADS, HEAD), jnp.float32), (key_blocks, value_blocks, pos_blocks))
        return (weighted.reshape(block_span, HEADS * HEAD).astype(jnp.bfloat16), row_lse)
    attn_blocks, lse_blocks = lax.map(per_query, (query_blocks, pos_blocks))
    return (attn_blocks.reshape(LENGTH, HEADS * HEAD), lse_blocks)

def attention_backward(query, keys, values, positions, grad_attn, attn, lse_blocks):
    block_span = math.gcd(LENGTH, 2048)
    block_count = LENGTH // block_span
    scale = HEAD ** (-0.5)
    delta = lax.optimization_barrier(jnp.sum(heads_of(grad_attn) * heads_of(attn), axis=-1))
    delta_blocks = jnp.transpose(blocked(delta, block_span), (0, 2, 1))
    query_blocks = blocked(query, block_span)
    grad_blocks = blocked(grad_attn, block_span)
    key_blocks = blocked(keys, block_span)
    value_blocks = blocked(values, block_span)
    pos_blocks = blocked(positions, block_span)

    def per_key(grad_query, key_args):
        key_block, value_block, key_pos = key_args
        key_heads = heads_of(key_block)
        value_heads = heads_of(value_block)

        def per_query(key_grads, query_args):
            query_block, grad_block, lse_block, delta_block, query_pos = query_args
            scores, allowed = tile_scores(query_block, query_pos, key_block, key_pos)
            probs = jnp.where(allowed, jnp.exp(scores - lse_block[..., None]), 0.0)
            grad_heads = heads_of(grad_block)
            grad_values = jnp.einsum('hrk,rhd->khd', probs.astype(jnp.bfloat16).astype(jnp.float32), grad_heads)
            grad_probs = jnp.einsum('rhd,khd->hrk', grad_heads, value_heads)
            grad_scores = (probs * (grad_probs - delta_block[..., None])).astype(jnp.bfloat16).astype(jnp.float32)
            grad_q = jnp.einsum('hrk,khd->rhd', grad_scores, key_heads) * scale
            grad_k = jnp.einsum('hrk,rhd->khd', grad_scores, heads_of(query_block)) * scale
            return ((key_grads[0] + grad_k, key_grads[1] + grad_values), grad_q)
        initial = (jnp.zeros((block_span, HEADS, HEAD), jnp.float32), jnp.zeros((block_span, HEADS, HEAD), jnp.float32))
        key_grads, query_parts = lax.scan(per_query, initial, (query_blocks, grad_blocks, lse_blocks, delta_blocks, pos_blocks))
        return (grad_query + query_parts, key_grads)
    grad_query, key_grads = lax.scan(per_key, jnp.zeros((block_count, block_span, HEADS, HEAD), jnp.float32), (key_blocks, value_blocks, pos_blocks))
    width = HEADS * HEAD
    return (grad_query.reshape(LENGTH, width), key_grads[0].reshape(LENGTH, width), key_grads[1].reshape(LENGTH, width))

def reference(block_input, positions, norm1_gain, norm1_bias, qkv_weight, query_bias, value_bias, proj_weight, proj_bias, norm2_gain, norm2_bias, fc_weight, fc_bias, out_weight, out_bias, cotangent):
    residual = block_input.astype(jnp.float32)
    normed1_out, normed1, inv_std1 = layer_norm(residual, norm1_gain, norm1_bias)
    norm1 = normed1_out.astype(jnp.bfloat16)
    qkv = jnp.dot(norm1, qkv_weight, preferred_element_type=jnp.float32)
    query = (qkv[:, :D] + query_bias.astype(jnp.float32)).astype(jnp.bfloat16)
    keys = qkv[:, D:2 * D].astype(jnp.bfloat16)
    values = (qkv[:, 2 * D:] + value_bias.astype(jnp.float32)).astype(jnp.bfloat16)
    attn, lse_blocks = attention_forward(query, keys, values, positions)
    middle = residual + jnp.dot(attn, proj_weight, preferred_element_type=jnp.float32) + proj_bias.astype(jnp.float32)
    normed2_out, normed2, inv_std2 = layer_norm(middle, norm2_gain, norm2_bias)
    norm2 = normed2_out.astype(jnp.bfloat16)
    pre_act = jnp.dot(norm2, fc_weight, preferred_element_type=jnp.float32) + fc_bias.astype(jnp.float32)
    act = gelu_forward(pre_act).astype(jnp.bfloat16)
    block_output = middle + jnp.dot(act, out_weight, preferred_element_type=jnp.float32) + out_bias.astype(jnp.float32)
    grad_out = cotangent.astype(jnp.float32)
    out_weight_grad = jnp.dot(act.T, cotangent, preferred_element_type=jnp.float32)
    out_bias_grad = lax.optimization_barrier(jnp.sum(grad_out, axis=0))
    grad_act = jnp.dot(cotangent, out_weight.T, preferred_element_type=jnp.float32)
    grad_pre = grad_act * gelu_slope(pre_act)
    fc_bias_grad = lax.optimization_barrier(jnp.sum(grad_pre, axis=0))
    grad_pre_half = grad_pre.astype(jnp.bfloat16)
    fc_weight_grad = jnp.dot(norm2.T, grad_pre_half, preferred_element_type=jnp.float32)
    grad_norm2 = jnp.dot(grad_pre_half, fc_weight.T, preferred_element_type=jnp.float32)
    norm2_gain_grad = lax.optimization_barrier(jnp.sum(grad_norm2 * normed2, axis=0))
    norm2_bias_grad = lax.optimization_barrier(jnp.sum(grad_norm2, axis=0))
    grad_middle = grad_out + norm_backward(grad_norm2, norm2_gain, normed2, inv_std2)
    proj_bias_grad = lax.optimization_barrier(jnp.sum(grad_middle, axis=0))
    grad_middle_half = grad_middle.astype(jnp.bfloat16)
    proj_weight_grad = jnp.dot(attn.T, grad_middle_half, preferred_element_type=jnp.float32)
    grad_attn = jnp.dot(grad_middle_half, proj_weight.T, preferred_element_type=jnp.float32).astype(jnp.bfloat16)
    grad_query, grad_keys, grad_values = attention_backward(query, keys, values, positions, grad_attn, attn, lse_blocks)
    query_bias_grad = lax.optimization_barrier(jnp.sum(grad_query, axis=0))
    value_bias_grad = lax.optimization_barrier(jnp.sum(grad_values, axis=0))
    grad_qkv = jnp.concatenate([grad_query, grad_keys, grad_values], axis=1).astype(jnp.bfloat16)
    qkv_weight_grad = jnp.dot(norm1.T, grad_qkv, preferred_element_type=jnp.float32)
    grad_norm1 = jnp.dot(grad_qkv, qkv_weight.T, preferred_element_type=jnp.float32)
    norm1_gain_grad = lax.optimization_barrier(jnp.sum(grad_norm1 * normed1, axis=0))
    norm1_bias_grad = lax.optimization_barrier(jnp.sum(grad_norm1, axis=0))
    input_grad = grad_middle + norm_backward(grad_norm1, norm1_gain, normed1, inv_std1)
    return (block_output, input_grad, norm1_gain_grad, norm1_bias_grad, qkv_weight_grad, query_bias_grad, value_bias_grad, proj_weight_grad, proj_bias_grad, norm2_gain_grad, norm2_bias_grad, fc_weight_grad, fc_bias_grad, out_weight_grad, out_bias_grad)
```

```python
import functools

import jax
import jax.numpy as jnp
from jax import lax
from jax.experimental import pallas as pl
from jax.experimental.pallas import tpu as pltpu
from jax.sharding import PartitionSpec as P

HEADS = 12
HEAD = 64


EPSILON = 1e-05
NEG_FILL = -1e30
GELU_C = 0.7978845608028654
GELU_K = 0.044715


def passed_along(block, axis, distance):
    devices = range(lax.axis_size(axis))
    route = [((i - distance) % len(devices), i) for i in devices]
    return lax.ppermute(block, axis, route)


def layer_norm(values_in, gain, shift):
    row_mean = jnp.mean(values_in, axis=-1, keepdims=True)
    centered = values_in - row_mean
    variance = jnp.mean(centered * centered, axis=-1, keepdims=True)
    inv_std = lax.rsqrt(variance + EPSILON)
    normed = centered * inv_std
    return (normed * gain.astype(jnp.float32) + shift.astype(jnp.float32), normed, inv_std)


def norm_backward(grad_norm, gain, normed, inv_std):
    scaled = grad_norm * gain.astype(jnp.float32)
    scaled_mean = jnp.mean(scaled, axis=-1, keepdims=True)
    cross_mean = jnp.mean(scaled * normed, axis=-1, keepdims=True)
    return inv_std * (scaled - scaled_mean - normed * cross_mean)


def gelu_forward(pre_act):
    cubed = pre_act * pre_act * pre_act
    return 0.5 * pre_act * (1.0 + jnp.tanh(GELU_C * (pre_act + GELU_K * cubed)))


def gelu_slope(pre_act):
    cubed = pre_act * pre_act * pre_act
    tanh_value = jnp.tanh(GELU_C * (pre_act + GELU_K * cubed))
    return 0.5 * (1.0 + tanh_value) + 0.5 * pre_act * (1.0 - tanh_value * tanh_value) * GELU_C * (
        1.0 + 3.0 * GELU_K * pre_act * pre_act
    )


def rows_product(left, right):
    return lax.dot_general(
        left, right, (((0,), (0,)), ((), ())), preferred_element_type=jnp.float32
    )


def transposed_product(left, right):
    return lax.dot_general(
        left, right, (((1,), (1,)), ((), ())), preferred_element_type=jnp.float32
    )


def split_heads(matrix):
    return matrix.reshape(matrix.shape[0], HEADS, HEAD)


def masked_scores(query, query_pos, keys, key_pos):
    scores = jnp.einsum(
        "rhd,khd->hrk", split_heads(query), split_heads(keys), preferred_element_type=jnp.float32
    ) * HEAD ** (-0.5)
    allowed = (key_pos[None, :] <= query_pos[:, None])[None]
    return (jnp.where(allowed, scores, NEG_FILL), allowed)


def attend_block(carried, query, query_pos, keys, values, key_pos):
    weighted, run_max, row_total = carried
    scores, allowed = masked_scores(query, query_pos, keys, key_pos)
    new_max = jnp.maximum(run_max, jnp.max(scores, axis=-1))
    weights = jnp.where(allowed, jnp.exp(scores - new_max[..., None]), 0.0)
    factor = jnp.exp(run_max - new_max)
    row_total = row_total * factor + jnp.sum(weights, axis=-1)
    update = jnp.einsum(
        "hrk,khd->rhd",
        weights,
        split_heads(values).astype(jnp.float32),
        precision=lax.Precision.HIGHEST,
        preferred_element_type=jnp.float32,
    )
    weighted = weighted * factor.T[:, :, None] + update
    return (weighted, new_max, row_total)


def attend_tile(carried, query, query_pos, keys, values, key_pos):
    half_rows = keys.shape[0] // 2
    latest = jnp.max(query_pos)
    for half_index in range(2):
        first_row = half_index * half_rows
        part_keys = keys[first_row : first_row + half_rows]
        part_values = values[first_row : first_row + half_rows]
        part_pos = key_pos[first_row : first_row + half_rows]

        def keep_state(state_in, block_keys, block_values, block_pos):
            return state_in

        def update_state(state_in, block_keys, block_values, block_pos):
            return attend_block(state_in, query, query_pos, block_keys, block_values, block_pos)

        carried = lax.cond(
            jnp.min(part_pos) > latest,
            keep_state,
            update_state,
            carried,
            part_keys,
            part_values,
            part_pos,
        )
    return carried


def block_grads(query, grad_attn, row_lse, row_delta, query_pos, keys, values, key_pos):
    scores, allowed = masked_scores(query, query_pos, keys, key_pos)
    probs = jnp.where(allowed, jnp.exp(scores - row_lse[..., None]), 0.0)
    grad_heads = split_heads(grad_attn)
    grad_values = jnp.einsum(
        "hrk,rhd->khd", probs.astype(jnp.bfloat16), grad_heads, preferred_element_type=jnp.float32
    )
    grad_probs = jnp.einsum(
        "rhd,khd->hrk", grad_heads, split_heads(values), preferred_element_type=jnp.float32
    )
    grad_scores = (probs * (grad_probs - row_delta[..., None])).astype(jnp.bfloat16)
    scale = HEAD ** (-0.5)
    grad_query = (
        jnp.einsum(
            "hrk,khd->rhd", grad_scores, split_heads(keys), preferred_element_type=jnp.float32
        )
        * scale
    )
    grad_keys = (
        jnp.einsum(
            "hrk,rhd->khd", grad_scores, split_heads(query), preferred_element_type=jnp.float32
        )
        * scale
    )
    key_rows = keys.shape[0]
    return (grad_query, grad_keys.reshape(key_rows, -1), grad_values.reshape(key_rows, -1))


def tile_grads(query, grad_attn, row_lse, row_delta, query_pos, keys, values, key_pos):
    half_rows = keys.shape[0] // 2
    key_width = keys.shape[1]
    latest = jnp.max(query_pos)
    query_total = jnp.zeros((query.shape[0], HEADS, HEAD), jnp.float32)
    key_parts = []
    value_parts = []
    for half_index in range(2):
        first_row = half_index * half_rows
        part_keys = keys[first_row : first_row + half_rows]
        part_values = values[first_row : first_row + half_rows]
        part_pos = key_pos[first_row : first_row + half_rows]

        def skipped(block_keys, block_values, block_pos):
            return (
                jnp.zeros((query.shape[0], HEADS, HEAD), jnp.float32),
                jnp.zeros((half_rows, key_width), jnp.float32),
                jnp.zeros((half_rows, key_width), jnp.float32),
            )

        def computed(block_keys, block_values, block_pos):
            return block_grads(
                query, grad_attn, row_lse, row_delta, query_pos, block_keys, block_values, block_pos
            )

        step_query, step_keys, step_values = lax.cond(
            jnp.min(part_pos) > latest, skipped, computed, part_keys, part_values, part_pos
        )
        query_total = query_total + step_query
        key_parts.append(step_keys)
        value_parts.append(step_values)
    return (query_total, jnp.concatenate(key_parts, axis=0), jnp.concatenate(value_parts, axis=0))


def shards(
    block_input,
    positions,
    norm1_gain,
    norm1_bias,
    qkv_weight,
    query_bias,
    value_bias,
    proj_weight,
    proj_bias,
    norm2_gain,
    norm2_bias,
    fc_weight,
    fc_bias,
    out_weight,
    out_bias,
    cotangent,
):
    rows = block_input.shape[0]
    width = block_input.shape[1]
    ctx_size = lax.axis_size("ctx")
    shard_count = lax.axis_size("fsdp")
    ctx_index = lax.axis_index("ctx")
    shard_index = lax.axis_index("fsdp")
    group_rows = rows * shard_count

    def key_positions(source):
        return lax.dynamic_slice_in_dim(positions, source * group_rows, group_rows)

    gain_one, shift_one, qkv_full, qbias_full, vbias_full, proj_full, pbias_full = (
        lax.all_gather(norm1_gain, "fsdp", axis=0, tiled=True),
        lax.all_gather(norm1_bias, "fsdp", axis=0, tiled=True),
        lax.all_gather(qkv_weight, "fsdp", axis=0, tiled=True),
        lax.all_gather(query_bias, "fsdp", axis=0, tiled=True),
        lax.all_gather(value_bias, "fsdp", axis=0, tiled=True),
        lax.all_gather(proj_weight, "fsdp", axis=0, tiled=True),
        lax.all_gather(proj_bias, "fsdp", axis=0, tiled=True),
    )
    gain_two, shift_two, fc_full, fbias_full, out_full, obias_full = (
        lax.all_gather(norm2_gain, "fsdp", axis=0, tiled=True),
        lax.all_gather(norm2_bias, "fsdp", axis=0, tiled=True),
        lax.all_gather(fc_weight, "fsdp", axis=0, tiled=True),
        lax.all_gather(fc_bias, "fsdp", axis=0, tiled=True),
        lax.all_gather(out_weight, "fsdp", axis=0, tiled=True),
        lax.all_gather(out_bias, "fsdp", axis=0, tiled=True),
    )
    residual = block_input.astype(jnp.float32)
    normed1_out, normed1, inv_std1 = layer_norm(residual, gain_one, shift_one)
    norm1 = normed1_out.astype(jnp.bfloat16)
    qkv = jnp.dot(norm1, qkv_full, preferred_element_type=jnp.float32)
    query = (qkv[:, :width] + qbias_full.astype(jnp.float32)).astype(jnp.bfloat16)
    keys = qkv[:, width : 2 * width].astype(jnp.bfloat16)
    values = (qkv[:, 2 * width :] + vbias_full.astype(jnp.float32)).astype(jnp.bfloat16)
    group_keys, group_values = (
        lax.all_gather(keys, "fsdp", axis=0, tiled=True),
        lax.all_gather(values, "fsdp", axis=0, tiled=True),
    )
    own_qpos = lax.dynamic_slice_in_dim(
        positions, (ctx_index * shard_count + shard_index) * rows, rows
    )
    own_kpos = key_positions(ctx_index)
    initial = (
        jnp.zeros((rows, HEADS, HEAD), jnp.float32),
        jnp.full((HEADS, rows), NEG_FILL, jnp.float32),
        jnp.zeros((HEADS, rows), jnp.float32),
    )
    carried = attend_tile(initial, query, own_qpos, group_keys, group_values, own_kpos)

    def forward_hop(hop_index, loop_carry):
        state_now, cycle_keys, cycle_values = loop_carry
        cycle_keys, cycle_values = passed_along((cycle_keys, cycle_values), "ctx", 1)
        source = (ctx_index - hop_index) % ctx_size
        state_now = attend_tile(
            state_now, query, own_qpos, cycle_keys, cycle_values, key_positions(source)
        )
        return (state_now, cycle_keys, cycle_values)

    result = lax.fori_loop(1, ctx_size, forward_hop, (carried, group_keys, group_values))
    carried = result[0]
    weighted, run_max, row_total = carried
    attn = (weighted / row_total.T[:, :, None]).reshape(rows, width).astype(jnp.bfloat16)
    row_lse = run_max + jnp.log(row_total)
    middle = (
        residual
        + jnp.dot(attn, proj_full, preferred_element_type=jnp.float32)
        + pbias_full.astype(jnp.float32)
    )
    normed2_out, normed2, inv_std2 = layer_norm(middle, gain_two, shift_two)
    norm2 = normed2_out.astype(jnp.bfloat16)
    pre_act = jnp.dot(norm2, fc_full, preferred_element_type=jnp.float32) + fbias_full.astype(
        jnp.float32
    )
    act = gelu_forward(pre_act).astype(jnp.bfloat16)
    block_output = (
        middle
        + jnp.dot(act, out_full, preferred_element_type=jnp.float32)
        + obias_full.astype(jnp.float32)
    )
    grad_out = cotangent.astype(jnp.float32)
    out_weight_grad = rows_product(act, cotangent)
    out_bias_grad = jnp.sum(grad_out, axis=0)
    grad_act = transposed_product(cotangent, out_full)
    grad_pre = grad_act * gelu_slope(pre_act)
    fc_bias_grad = jnp.sum(grad_pre, axis=0)
    grad_pre_half = grad_pre.astype(jnp.bfloat16)
    fc_weight_grad = rows_product(norm2, grad_pre_half)
    grad_norm2 = transposed_product(grad_pre_half, fc_full)
    norm2_gain_grad = jnp.sum(grad_norm2 * normed2, axis=0)
    norm2_bias_grad = jnp.sum(grad_norm2, axis=0)
    grad_middle = grad_out + norm_backward(grad_norm2, gain_two, normed2, inv_std2)
    mlp_shares = (
        lax.psum_scatter(norm2_gain_grad, "fsdp", scatter_dimension=0, tiled=True),
        lax.psum_scatter(norm2_bias_grad, "fsdp", scatter_dimension=0, tiled=True),
        lax.psum_scatter(fc_weight_grad, "fsdp", scatter_dimension=0, tiled=True),
        lax.psum_scatter(fc_bias_grad, "fsdp", scatter_dimension=0, tiled=True),
        lax.psum_scatter(out_weight_grad, "fsdp", scatter_dimension=0, tiled=True),
        lax.psum_scatter(out_bias_grad, "fsdp", scatter_dimension=0, tiled=True),
    )
    proj_bias_grad = jnp.sum(grad_middle, axis=0)
    grad_middle_half = grad_middle.astype(jnp.bfloat16)
    proj_weight_grad = rows_product(attn, grad_middle_half)
    grad_attn = transposed_product(grad_middle_half, proj_full).astype(jnp.bfloat16)
    row_delta = jnp.sum(
        split_heads(grad_attn).astype(jnp.float32) * split_heads(attn).astype(jnp.float32), axis=-1
    ).T
    grad_query, grad_keys, grad_values = tile_grads(
        query, grad_attn, row_lse, row_delta, own_qpos, group_keys, group_values, own_kpos
    )

    def pass_key_grads(key_grads):
        return passed_along((key_grads[0], key_grads[1]), "ctx", 1)

    def backward_hop(hop_index, loop_carry):
        query_sum, key_grads, cycle_keys, cycle_values = loop_carry
        cycle_keys, cycle_values = passed_along((cycle_keys, cycle_values), "ctx", 1)
        key_grads = pass_key_grads(key_grads)
        source = (ctx_index - hop_index) % ctx_size
        step_query, step_keys, step_values = tile_grads(
            query,
            grad_attn,
            row_lse,
            row_delta,
            own_qpos,
            cycle_keys,
            cycle_values,
            key_positions(source),
        )
        return (
            query_sum + step_query,
            (key_grads[0] + step_keys, key_grads[1] + step_values),
            cycle_keys,
            cycle_values,
        )

    result = lax.fori_loop(
        1, ctx_size, backward_hop, (grad_query, (grad_keys, grad_values), group_keys, group_values)
    )
    grad_query = result[0]
    key_grads = pass_key_grads(result[1])
    own_key_grad, own_value_grad = (
        lax.psum_scatter(key_grads[0], "fsdp", scatter_dimension=0, tiled=True),
        lax.psum_scatter(key_grads[1], "fsdp", scatter_dimension=0, tiled=True),
    )
    grad_query_rows = grad_query.reshape(rows, width)
    query_bias_grad = jnp.sum(grad_query_rows, axis=0)
    value_bias_grad = jnp.sum(own_value_grad, axis=0)
    grad_qkv = jnp.concatenate([grad_query_rows, own_key_grad, own_value_grad], axis=1).astype(
        jnp.bfloat16
    )
    qkv_weight_grad = rows_product(norm1, grad_qkv)
    grad_norm1 = transposed_product(grad_qkv, qkv_full)
    norm1_gain_grad = jnp.sum(grad_norm1 * normed1, axis=0)
    norm1_bias_grad = jnp.sum(grad_norm1, axis=0)
    input_grad = grad_middle + norm_backward(grad_norm1, gain_one, normed1, inv_std1)
    attn_shares = (
        lax.psum_scatter(norm1_gain_grad, "fsdp", scatter_dimension=0, tiled=True),
        lax.psum_scatter(norm1_bias_grad, "fsdp", scatter_dimension=0, tiled=True),
        lax.psum_scatter(qkv_weight_grad, "fsdp", scatter_dimension=0, tiled=True),
        lax.psum_scatter(query_bias_grad, "fsdp", scatter_dimension=0, tiled=True),
        lax.psum_scatter(value_bias_grad, "fsdp", scatter_dimension=0, tiled=True),
        lax.psum_scatter(proj_weight_grad, "fsdp", scatter_dimension=0, tiled=True),
        lax.psum_scatter(proj_bias_grad, "fsdp", scatter_dimension=0, tiled=True),
    )
    totals = lax.psum(
        (
            attn_shares[0],
            attn_shares[1],
            attn_shares[2],
            attn_shares[3],
            attn_shares[4],
            attn_shares[5],
            attn_shares[6],
            mlp_shares[0],
            mlp_shares[1],
            mlp_shares[2],
            mlp_shares[3],
            mlp_shares[4],
            mlp_shares[5],
        ),
        "ctx",
    )
    return (
        block_output,
        input_grad,
        totals[0],
        totals[1],
        totals[2],
        totals[3],
        totals[4],
        totals[5],
        totals[6],
        totals[7],
        totals[8],
        totals[9],
        totals[10],
        totals[11],
        totals[12],
    )


def head_cols(head, offset=0):
    return slice(offset + head * HEAD, offset + (head + 1) * HEAD)


def tile_keep(block, key_block, query_block):
    key_row = lax.broadcasted_iota(jnp.int32, (block, block), 0)
    query_col = lax.broadcasted_iota(jnp.int32, (block, block), 1)
    return key_row <= query_col + jnp.where(key_block == query_block, 0, block)


def forward_kernel(
    heads, block, ids_ref, own_ref, q_ref, kv_ref, out_ref, lse_ref, max_ref, sum_ref, acc_ref
):
    span = heads * HEAD
    max_ref[...] = jnp.full_like(max_ref, NEG_FILL)
    sum_ref[...] = jnp.zeros_like(sum_ref)
    acc_ref[...] = jnp.zeros_like(acc_ref)

    def step(index, carry):
        first = pl.multiple_of(index * block, block)
        key_block = ids_ref[index]
        for part in range(2):
            cols = slice(part * block, (part + 1) * block)
            query_block = own_ref[part]

            @pl.when(key_block <= query_block)
            def _():
                keep = tile_keep(block, key_block, query_block)
                for head in range(heads):
                    k = kv_ref[pl.ds(first, block), head_cols(head)]
                    v = kv_ref[pl.ds(first, block), head_cols(head, span)]
                    q = q_ref[cols, head_cols(head)]
                    scores = jnp.where(keep, transposed_product(k, q), NEG_FILL)
                    old_max = max_ref[head : head + 1, cols]
                    new_max = jnp.maximum(old_max, jnp.max(scores, axis=0, keepdims=True))
                    weights = jnp.exp(scores - new_max)
                    factor = jnp.exp(old_max - new_max)
                    max_ref[head : head + 1, cols] = new_max
                    sum_ref[head : head + 1, cols] = sum_ref[
                        head : head + 1, cols
                    ] * factor + jnp.sum(weights, axis=0, keepdims=True)
                    acc_ref[head_cols(head), cols] = acc_ref[
                        head_cols(head), cols
                    ] * factor + rows_product(v, weights.astype(jnp.bfloat16))

        return carry

    lax.fori_loop(0, kv_ref.shape[0] // block, step, 0)
    for head in range(heads):
        total = sum_ref[head : head + 1, :]
        out_ref[head_cols(head), :] = (acc_ref[head_cols(head), :] / total).astype(out_ref.dtype)
        lse_ref[head : head + 1, :] = max_ref[head : head + 1, :] + jnp.log(total)


def backward_kernel(
    heads, block, ids_ref, own_ref, q_ref, kv_ref, do_ref, lse_ref, delta_ref, dq_ref, dkv_ref, acc_ref
):
    span = heads * HEAD
    dq_ref[...] = jnp.zeros_like(dq_ref)

    def step(index, carry):
        first = pl.multiple_of(index * block, block)
        key_block = ids_ref[index]
        acc_ref[...] = jnp.zeros_like(acc_ref)
        for part in range(2):
            cols = slice(part * block, (part + 1) * block)
            query_block = own_ref[part]

            @pl.when(key_block <= query_block)
            def _():
                keep = tile_keep(block, key_block, query_block)
                key_parts = []
                value_parts = []
                for head in range(heads):
                    k = kv_ref[pl.ds(first, block), head_cols(head)]
                    v = kv_ref[pl.ds(first, block), head_cols(head, span)]
                    q = q_ref[cols, head_cols(head)]
                    do = do_ref[cols, head_cols(head)]
                    scores = jnp.where(keep, transposed_product(k, q), NEG_FILL)
                    probs = jnp.exp(scores - lse_ref[head : head + 1, cols])
                    value_parts.append(
                        jnp.dot(
                            probs.astype(jnp.bfloat16), do, preferred_element_type=jnp.float32
                        )
                    )
                    grad_probs = transposed_product(v, do)
                    grad_scores = (
                        probs * (grad_probs - delta_ref[head : head + 1, cols])
                    ).astype(jnp.bfloat16)
                    key_parts.append(
                        jnp.dot(grad_scores, q, preferred_element_type=jnp.float32)
                    )
                    dq_ref[head_cols(head), cols] += rows_product(k, grad_scores)
                acc_ref[...] += jnp.concatenate(key_parts + value_parts, axis=1)

        dkv_ref[pl.ds(first, block), :] = acc_ref[...].astype(dkv_ref.dtype)
        return carry

    lax.fori_loop(0, kv_ref.shape[0] // block, step, 0)


SMEM = pltpu.SMEM
VMEM = pltpu.VMEM


def attention_forward(heads, block, ids, own, q, kv):
    group_rows, span = q.shape
    return pl.pallas_call(
        functools.partial(forward_kernel, heads, block),
        out_shape=(
            jax.ShapeDtypeStruct((span, group_rows), jnp.bfloat16),
            jax.ShapeDtypeStruct((heads, group_rows), jnp.float32),
        ),
        in_specs=[pl.BlockSpec(memory_space=SMEM)] * 2 + [pl.BlockSpec(memory_space=VMEM)] * 2,
        out_specs=(pl.BlockSpec(memory_space=VMEM),) * 2,
        scratch_shapes=[
            VMEM((heads, group_rows), jnp.float32),
            VMEM((heads, group_rows), jnp.float32),
            VMEM((span, group_rows), jnp.float32),
        ],
        cost_estimate=pl.CostEstimate(
            flops=2 * group_rows * kv.shape[0] * span,
            bytes_accessed=2 * kv.size,
            transcendentals=group_rows * kv.shape[0] * heads // 2,
        ),
        name="attention_forward",
    )(ids, own, q, kv)


def attention_backward(heads, block, ids, own, q, kv, do, lse, delta):
    group_rows, span = q.shape
    return pl.pallas_call(
        functools.partial(backward_kernel, heads, block),
        out_shape=(
            jax.ShapeDtypeStruct((span, group_rows), jnp.float32),
            jax.ShapeDtypeStruct(kv.shape, jnp.bfloat16),
        ),
        in_specs=[pl.BlockSpec(memory_space=SMEM)] * 2 + [pl.BlockSpec(memory_space=VMEM)] * 5,
        out_specs=(pl.BlockSpec(memory_space=VMEM),) * 2,
        scratch_shapes=[VMEM((block, 2 * span), jnp.float32)],
        cost_estimate=pl.CostEstimate(
            flops=5 * group_rows * kv.shape[0] * span,
            bytes_accessed=4 * kv.size,
            transcendentals=group_rows * kv.shape[0] * heads // 2,
        ),
        name="attention_backward",
    )(ids, own, q, kv, do, lse, delta)


def head_shards(
    block_input,
    positions,
    norm1_gain,
    norm1_bias,
    qkv_weight,
    query_bias,
    value_bias,
    proj_weight,
    proj_bias,
    norm2_gain,
    norm2_bias,
    fc_weight,
    fc_bias,
    out_weight,
    out_bias,
    cotangent,
):
    rows, width = block_input.shape
    ctx_size = lax.axis_size("ctx")
    members = lax.axis_size("fsdp")
    ctx_index = lax.axis_index("ctx")
    member = lax.axis_index("fsdp")
    group_rows = rows * members
    block = group_rows // 2
    span = width // members
    heads = HEADS // members
    hidden = fc_weight.shape[1] // members
    piece = span // ctx_size
    f32, b16 = jnp.float32, jnp.bfloat16

    def gathered(value, axis=0):
        return lax.all_gather(value, "fsdp", axis=axis, tiled=True)

    def scattered(value):
        return lax.psum_scatter(value, "fsdp", scatter_dimension=0, tiled=True)

    def exchanged(value):
        return lax.all_to_all(value, "fsdp", 0, 0, tiled=True)

    def own_rows(value):
        return lax.dynamic_slice_in_dim(value, member * rows, rows)

    input_all = gathered(block_input)
    qkv_cols = exchanged(
        qkv_weight.reshape(span, 3, members, span).transpose(2, 0, 1, 3).reshape(members, span, 3 * span)
    ).reshape(width, 3 * span)
    vectors = gathered(
        jnp.stack([norm1_gain, norm1_bias, proj_bias, norm2_gain, norm2_bias, out_bias]), axis=1
    )
    gain_one, shift_one, pbias, gain_two, shift_two, obias = (vectors[i] for i in range(6))
    proj_full = gathered(proj_weight)
    fc_cols = exchanged(fc_weight.reshape(span, members, hidden).transpose(1, 0, 2)).reshape(
        width, hidden
    )
    cotangent_all = gathered(cotangent)

    ids = positions.reshape(2 * ctx_size, block)[:, 0] // block
    own_ids = lax.dynamic_slice_in_dim(ids, 2 * ctx_index, 2)

    residual = input_all.astype(f32)
    norm1 = layer_norm(residual, gain_one, shift_one)[0].astype(b16)
    qkv = jnp.dot(norm1, qkv_cols, preferred_element_type=f32)
    query = (qkv[:, :span] + query_bias.astype(f32)).astype(b16)
    keys = qkv[:, span : 2 * span].astype(b16)
    values = (qkv[:, 2 * span :] + value_bias.astype(f32)).astype(b16)
    query = query * jnp.asarray(HEAD**-0.5, b16)
    all_kv = lax.all_gather(jnp.concatenate([keys, values], axis=1), "ctx", axis=0, tiled=True)
    attn_t, lse = attention_forward(heads, block, ids, own_ids, query, all_kv)
    attn_all_t = gathered(attn_t)
    middle_all = residual + rows_product(attn_all_t, proj_full) + pbias.astype(f32)
    norm2 = layer_norm(middle_all, gain_two, shift_two)[0].astype(b16)
    pre_act = jnp.dot(norm2, fc_cols, preferred_element_type=f32) + fc_bias.astype(f32)
    act = gelu_forward(pre_act).astype(b16)
    grad_act = transposed_product(cotangent_all, out_weight)
    grad_pre = grad_act * gelu_slope(pre_act)
    fc_bias_grad = jnp.sum(grad_pre, axis=0)
    grad_pre_half = grad_pre.astype(b16)
    grad_norm2 = scattered(transposed_product(grad_pre_half, fc_cols).astype(b16)).astype(f32)
    middle = own_rows(middle_all)
    _, normed2, inv_std2 = layer_norm(middle, gain_two, shift_two)
    grad_out = cotangent.astype(f32)
    grad_middle = grad_out + norm_backward(grad_norm2, gain_two, normed2, inv_std2)
    grad_middle_all = gathered(grad_middle.astype(b16))

    mlp_out = scattered(jnp.dot(act, out_weight, preferred_element_type=f32).astype(b16))
    block_output = middle + mlp_out.astype(f32) + obias.astype(f32)

    grad_attn = transposed_product(grad_middle_all, proj_weight).astype(b16)
    delta = jnp.sum(
        (grad_attn.T.astype(f32) * attn_t.astype(f32)).reshape(heads, HEAD, group_rows), axis=1
    )
    grad_query_t, grad_kv = attention_backward(
        heads, block, ids, own_ids, query, all_kv, grad_attn, lse, delta
    )
    own_kv = lax.psum_scatter(grad_kv, "ctx", scatter_dimension=0, tiled=True)

    out_weight_grad = rows_product(act, cotangent_all).astype(b16)
    fc_weight_grad = rows_product(norm2, grad_pre_half).astype(b16)
    proj_weight_grad = jnp.dot(attn_t, grad_middle_all, preferred_element_type=f32).astype(b16)
    shares = jnp.concatenate(
        [
            out_weight_grad.reshape(ctx_size, -1, width),
            proj_weight_grad.reshape(ctx_size, piece, width),
            fc_weight_grad.reshape(members, ctx_size, piece, hidden)
            .transpose(1, 0, 2, 3)
            .reshape(ctx_size, members * piece, hidden),
        ],
        axis=1,
    )
    shares = lax.psum_scatter(shares, "ctx", scatter_dimension=0, tiled=True)[0]
    kept = shares.shape[0] - members * piece
    shares = jnp.concatenate([shares[:kept], exchanged(shares[kept:])], axis=0)
    shares = lax.all_gather(shares, "ctx", axis=0, tiled=False)
    out_rows = out_weight.shape[0] // ctx_size
    out_weight_grad = shares[:, :out_rows].reshape(out_weight.shape).astype(f32)
    proj_weight_grad = shares[:, out_rows:kept].reshape(proj_weight.shape).astype(f32)
    fc_weight_grad = (
        shares[:, kept:]
        .reshape(ctx_size, members, piece, hidden)
        .transpose(0, 2, 1, 3)
        .reshape(fc_weight.shape)
        .astype(f32)
    )

    grad_query = grad_query_t.T * HEAD**-0.5
    grad_qkv = jnp.concatenate([grad_query.astype(b16), own_kv], axis=1)
    grad_norm1 = scattered(transposed_product(grad_qkv, qkv_cols).astype(b16)).astype(f32)
    qkv_share = rows_product(norm1, grad_qkv).astype(b16)
    qkv_share = (
        qkv_share.reshape(members, ctx_size, piece, 3 * span)
        .transpose(1, 0, 2, 3)
        .reshape(ctx_size, members * piece, 3 * span)
    )
    qkv_share = lax.psum_scatter(qkv_share, "ctx", scatter_dimension=0, tiled=True)[0]
    qkv_share = lax.all_gather(exchanged(qkv_share), "ctx", axis=0, tiled=False)
    qkv_weight_grad = (
        qkv_share.reshape(ctx_size, members, piece, 3, span)
        .transpose(0, 2, 3, 1, 4)
        .reshape(qkv_weight.shape)
        .astype(f32)
    )
    _, normed1, inv_std1 = layer_norm(block_input.astype(f32), gain_one, shift_one)
    input_grad = grad_middle + norm_backward(grad_norm1, gain_one, normed1, inv_std1)

    split_sums = jnp.concatenate(
        [
            jnp.sum(grad_query, axis=0),
            jnp.sum(own_kv[:, span:].astype(f32), axis=0),
            fc_bias_grad,
        ]
    )
    row_sums = jnp.stack(
        [
            jnp.sum(grad_norm1 * normed1, axis=0),
            jnp.sum(grad_norm1, axis=0),
            jnp.sum(grad_middle, axis=0),
            jnp.sum(grad_norm2 * normed2, axis=0),
            jnp.sum(grad_norm2, axis=0),
            jnp.sum(grad_out, axis=0),
        ]
    ).reshape(6, members, span)
    own_slot = (jnp.arange(members) == member)[:, None]
    sums = jnp.concatenate(
        [
            row_sums.transpose(1, 0, 2).reshape(members, 6 * span),
            jnp.where(own_slot, split_sums[None], 0.0),
        ],
        axis=1,
    )
    sums = lax.dynamic_index_in_dim(lax.psum(sums, ("ctx", "fsdp")), member, keepdims=False)
    parts = sums[: 8 * span].reshape(8, span)
    return (
        block_output,
        input_grad,
        parts[0],
        parts[1],
        qkv_weight_grad,
        parts[6],
        parts[7],
        proj_weight_grad,
        parts[2],
        parts[3],
        parts[4],
        fc_weight_grad,
        sums[8 * span :],
        out_weight_grad,
        parts[5],
    )


def solution(mesh):
    in_specs = (
        P(("ctx", "fsdp"), None),
        P(),
        P("fsdp"),
        P("fsdp"),
        P("fsdp", None),
        P("fsdp"),
        P("fsdp"),
        P("fsdp", None),
        P("fsdp"),
        P("fsdp"),
        P("fsdp"),
        P("fsdp", None),
        P("fsdp"),
        P("fsdp", None),
        P("fsdp"),
        P(("ctx", "fsdp"), None),
    )
    out_specs = (
        P(("ctx", "fsdp"), None),
        P(("ctx", "fsdp"), None),
        P("fsdp"),
        P("fsdp"),
        P("fsdp", None),
        P("fsdp"),
        P("fsdp"),
        P("fsdp", None),
        P("fsdp"),
        P("fsdp"),
        P("fsdp"),
        P("fsdp", None),
        P("fsdp"),
        P("fsdp", None),
        P("fsdp"),
    )
    members = mesh.shape["fsdp"]
    by_heads = HEADS % members == 0 and (HEADS // members * HEAD) % mesh.shape["ctx"] == 0
    body = head_shards if by_heads else shards
    return jax.shard_map(body, mesh=mesh, in_specs=in_specs, out_specs=out_specs, check_vma=False)
```

```python
import functools

import jax
import jax.numpy as jnp
from jax import lax
from jax.experimental import pallas as pl
from jax.experimental.pallas import tpu as pltpu
from jax.sharding import PartitionSpec as P

HEADS = 12
HEAD = 64


EPSILON = 1e-05
NEG_FILL = -1e30
GELU_C = 0.7978845608028654
GELU_K = 0.044715


def passed_along(block, axis, distance):
    devices = range(lax.axis_size(axis))
    route = [((i - distance) % len(devices), i) for i in devices]
    return lax.ppermute(block, axis, route)


def layer_norm(values_in, gain, shift):
    row_mean = jnp.mean(values_in, axis=-1, keepdims=True)
    centered = values_in - row_mean
    variance = jnp.mean(centered * centered, axis=-1, keepdims=True)
    inv_std = lax.rsqrt(variance + EPSILON)
    normed = centered * inv_std
    return (normed * gain.astype(jnp.float32) + shift.astype(jnp.float32), normed, inv_std)


def norm_backward(grad_norm, gain, normed, inv_std):
    scaled = grad_norm * gain.astype(jnp.float32)
    scaled_mean = jnp.mean(scaled, axis=-1, keepdims=True)
    cross_mean = jnp.mean(scaled * normed, axis=-1, keepdims=True)
    return inv_std * (scaled - scaled_mean - normed * cross_mean)


def gelu_forward(pre_act):
    cubed = pre_act * pre_act * pre_act
    return 0.5 * pre_act * (1.0 + jnp.tanh(GELU_C * (pre_act + GELU_K * cubed)))


def gelu_slope(pre_act):
    cubed = pre_act * pre_act * pre_act
    tanh_value = jnp.tanh(GELU_C * (pre_act + GELU_K * cubed))
    return 0.5 * (1.0 + tanh_value) + 0.5 * pre_act * (1.0 - tanh_value * tanh_value) * GELU_C * (
        1.0 + 3.0 * GELU_K * pre_act * pre_act
    )


def rows_product(left, right):
    return lax.dot_general(
        left, right, (((0,), (0,)), ((), ())), preferred_element_type=jnp.float32
    )


def transposed_product(left, right):
    return lax.dot_general(
        left, right, (((1,), (1,)), ((), ())), preferred_element_type=jnp.float32
    )


def split_heads(matrix):
    return matrix.reshape(matrix.shape[0], HEADS, HEAD)


def masked_scores(query, query_pos, keys, key_pos):
    scores = jnp.einsum(
        "rhd,khd->hrk", split_heads(query), split_heads(keys), preferred_element_type=jnp.float32
    ) * HEAD ** (-0.5)
    allowed = (key_pos[None, :] <= query_pos[:, None])[None]
    return (jnp.where(allowed, scores, NEG_FILL), allowed)


def attend_block(carried, query, query_pos, keys, values, key_pos):
    weighted, run_max, row_total = carried
    scores, allowed = masked_scores(query, query_pos, keys, key_pos)
    new_max = jnp.maximum(run_max, jnp.max(scores, axis=-1))
    weights = jnp.where(allowed, jnp.exp(scores - new_max[..., None]), 0.0)
    factor = jnp.exp(run_max - new_max)
    row_total = row_total * factor + jnp.sum(weights, axis=-1)
    update = jnp.einsum(
        "hrk,khd->rhd",
        weights,
        split_heads(values).astype(jnp.float32),
        precision=lax.Precision.HIGHEST,
        preferred_element_type=jnp.float32,
    )
    weighted = weighted * factor.T[:, :, None] + update
    return (weighted, new_max, row_total)


def attend_tile(carried, query, query_pos, keys, values, key_pos):
    half_rows = keys.shape[0] // 2
    latest = jnp.max(query_pos)
    for half_index in range(2):
        first_row = half_index * half_rows
        part_keys = keys[first_row : first_row + half_rows]
        part_values = values[first_row : first_row + half_rows]
        part_pos = key_pos[first_row : first_row + half_rows]

        def keep_state(state_in, block_keys, block_values, block_pos):
            return state_in

        def update_state(state_in, block_keys, block_values, block_pos):
            return attend_block(state_in, query, query_pos, block_keys, block_values, block_pos)

        carried = lax.cond(
            jnp.min(part_pos) > latest,
            keep_state,
            update_state,
            carried,
            part_keys,
            part_values,
            part_pos,
        )
    return carried


def block_grads(query, grad_attn, row_lse, row_delta, query_pos, keys, values, key_pos):
    scores, allowed = masked_scores(query, query_pos, keys, key_pos)
    probs = jnp.where(allowed, jnp.exp(scores - row_lse[..., None]), 0.0)
    grad_heads = split_heads(grad_attn)
    grad_values = jnp.einsum(
        "hrk,rhd->khd", probs.astype(jnp.bfloat16), grad_heads, preferred_element_type=jnp.float32
    )
    grad_probs = jnp.einsum(
        "rhd,khd->hrk", grad_heads, split_heads(values), preferred_element_type=jnp.float32
    )
    grad_scores = (probs * (grad_probs - row_delta[..., None])).astype(jnp.bfloat16)
    scale = HEAD ** (-0.5)
    grad_query = (
        jnp.einsum(
            "hrk,khd->rhd", grad_scores, split_heads(keys), preferred_element_type=jnp.float32
        )
        * scale
    )
    grad_keys = (
        jnp.einsum(
            "hrk,rhd->khd", grad_scores, split_heads(query), preferred_element_type=jnp.float32
        )
        * scale
    )
    key_rows = keys.shape[0]
    return (grad_query, grad_keys.reshape(key_rows, -1), grad_values.reshape(key_rows, -1))


def tile_grads(query, grad_attn, row_lse, row_delta, query_pos, keys, values, key_pos):
    half_rows = keys.shape[0] // 2
    key_width = keys.shape[1]
    latest = jnp.max(query_pos)
    query_total = jnp.zeros((query.shape[0], HEADS, HEAD), jnp.float32)
    key_parts = []
    value_parts = []
    for half_index in range(2):
        first_row = half_index * half_rows
        part_keys = keys[first_row : first_row + half_rows]
        part_values = values[first_row : first_row + half_rows]
        part_pos = key_pos[first_row : first_row + half_rows]

        def skipped(block_keys, block_values, block_pos):
            return (
                jnp.zeros((query.shape[0], HEADS, HEAD), jnp.float32),
                jnp.zeros((half_rows, key_width), jnp.float32),
                jnp.zeros((half_rows, key_width), jnp.float32),
            )

        def computed(block_keys, block_values, block_pos):
            return block_grads(
                query, grad_attn, row_lse, row_delta, query_pos, block_keys, block_values, block_pos
            )

        step_query, step_keys, step_values = lax.cond(
            jnp.min(part_pos) > latest, skipped, computed, part_keys, part_values, part_pos
        )
        query_total = query_total + step_query
        key_parts.append(step_keys)
        value_parts.append(step_values)
    return (query_total, jnp.concatenate(key_parts, axis=0), jnp.concatenate(value_parts, axis=0))


def shards(
    block_input,
    positions,
    norm1_gain,
    norm1_bias,
    qkv_weight,
    query_bias,
    value_bias,
    proj_weight,
    proj_bias,
    norm2_gain,
    norm2_bias,
    fc_weight,
    fc_bias,
    out_weight,
    out_bias,
    cotangent,
):
    rows = block_input.shape[0]
    width = block_input.shape[1]
    ctx_size = lax.axis_size("ctx")
    shard_count = lax.axis_size("fsdp")
    ctx_index = lax.axis_index("ctx")
    shard_index = lax.axis_index("fsdp")
    group_rows = rows * shard_count

    def key_positions(source):
        return lax.dynamic_slice_in_dim(positions, source * group_rows, group_rows)

    gain_one, shift_one, qkv_full, qbias_full, vbias_full, proj_full, pbias_full = (
        lax.all_gather(norm1_gain, "fsdp", axis=0, tiled=True),
        lax.all_gather(norm1_bias, "fsdp", axis=0, tiled=True),
        lax.all_gather(qkv_weight, "fsdp", axis=0, tiled=True),
        lax.all_gather(query_bias, "fsdp", axis=0, tiled=True),
        lax.all_gather(value_bias, "fsdp", axis=0, tiled=True),
        lax.all_gather(proj_weight, "fsdp", axis=0, tiled=True),
        lax.all_gather(proj_bias, "fsdp", axis=0, tiled=True),
    )
    gain_two, shift_two, fc_full, fbias_full, out_full, obias_full = (
        lax.all_gather(norm2_gain, "fsdp", axis=0, tiled=True),
        lax.all_gather(norm2_bias, "fsdp", axis=0, tiled=True),
        lax.all_gather(fc_weight, "fsdp", axis=0, tiled=True),
        lax.all_gather(fc_bias, "fsdp", axis=0, tiled=True),
        lax.all_gather(out_weight, "fsdp", axis=0, tiled=True),
        lax.all_gather(out_bias, "fsdp", axis=0, tiled=True),
    )
    residual = block_input.astype(jnp.float32)
    normed1_out, normed1, inv_std1 = layer_norm(residual, gain_one, shift_one)
    norm1 = normed1_out.astype(jnp.bfloat16)
    qkv = jnp.dot(norm1, qkv_full, preferred_element_type=jnp.float32)
    query = (qkv[:, :width] + qbias_full.astype(jnp.float32)).astype(jnp.bfloat16)
    keys = qkv[:, width : 2 * width].astype(jnp.bfloat16)
    values = (qkv[:, 2 * width :] + vbias_full.astype(jnp.float32)).astype(jnp.bfloat16)
    group_keys, group_values = (
        lax.all_gather(keys, "fsdp", axis=0, tiled=True),
        lax.all_gather(values, "fsdp", axis=0, tiled=True),
    )
    own_qpos = lax.dynamic_slice_in_dim(
        positions, (ctx_index * shard_count + shard_index) * rows, rows
    )
    own_kpos = key_positions(ctx_index)
    initial = (
        jnp.zeros((rows, HEADS, HEAD), jnp.float32),
        jnp.full((HEADS, rows), NEG_FILL, jnp.float32),
        jnp.zeros((HEADS, rows), jnp.float32),
    )
    carried = attend_tile(initial, query, own_qpos, group_keys, group_values, own_kpos)

    def forward_hop(hop_index, loop_carry):
        state_now, cycle_keys, cycle_values = loop_carry
        cycle_keys, cycle_values = passed_along((cycle_keys, cycle_values), "ctx", 1)
        source = (ctx_index - hop_index) % ctx_size
        state_now = attend_tile(
            state_now, query, own_qpos, cycle_keys, cycle_values, key_positions(source)
        )
        return (state_now, cycle_keys, cycle_values)

    result = lax.fori_loop(1, ctx_size, forward_hop, (carried, group_keys, group_values))
    carried = result[0]
    weighted, run_max, row_total = carried
    attn = (weighted / row_total.T[:, :, None]).reshape(rows, width).astype(jnp.bfloat16)
    row_lse = run_max + jnp.log(row_total)
    middle = (
        residual
        + jnp.dot(attn, proj_full, preferred_element_type=jnp.float32)
        + pbias_full.astype(jnp.float32)
    )
    normed2_out, normed2, inv_std2 = layer_norm(middle, gain_two, shift_two)
    norm2 = normed2_out.astype(jnp.bfloat16)
    pre_act = jnp.dot(norm2, fc_full, preferred_element_type=jnp.float32) + fbias_full.astype(
        jnp.float32
    )
    act = gelu_forward(pre_act).astype(jnp.bfloat16)
    block_output = (
        middle
        + jnp.dot(act, out_full, preferred_element_type=jnp.float32)
        + obias_full.astype(jnp.float32)
    )
    grad_out = cotangent.astype(jnp.float32)
    out_weight_grad = rows_product(act, cotangent)
    out_bias_grad = jnp.sum(grad_out, axis=0)
    grad_act = transposed_product(cotangent, out_full)
    grad_pre = grad_act * gelu_slope(pre_act)
    fc_bias_grad = jnp.sum(grad_pre, axis=0)
    grad_pre_half = grad_pre.astype(jnp.bfloat16)
    fc_weight_grad = rows_product(norm2, grad_pre_half)
    grad_norm2 = transposed_product(grad_pre_half, fc_full)
    norm2_gain_grad = jnp.sum(grad_norm2 * normed2, axis=0)
    norm2_bias_grad = jnp.sum(grad_norm2, axis=0)
    grad_middle = grad_out + norm_backward(grad_norm2, gain_two, normed2, inv_std2)
    mlp_shares = (
        lax.psum_scatter(norm2_gain_grad, "fsdp", scatter_dimension=0, tiled=True),
        lax.psum_scatter(norm2_bias_grad, "fsdp", scatter_dimension=0, tiled=True),
        lax.psum_scatter(fc_weight_grad, "fsdp", scatter_dimension=0, tiled=True),
        lax.psum_scatter(fc_bias_grad, "fsdp", scatter_dimension=0, tiled=True),
        lax.psum_scatter(out_weight_grad, "fsdp", scatter_dimension=0, tiled=True),
        lax.psum_scatter(out_bias_grad, "fsdp", scatter_dimension=0, tiled=True),
    )
    proj_bias_grad = jnp.sum(grad_middle, axis=0)
    grad_middle_half = grad_middle.astype(jnp.bfloat16)
    proj_weight_grad = rows_product(attn, grad_middle_half)
    grad_attn = transposed_product(grad_middle_half, proj_full).astype(jnp.bfloat16)
    row_delta = jnp.sum(
        split_heads(grad_attn).astype(jnp.float32) * split_heads(attn).astype(jnp.float32), axis=-1
    ).T
    grad_query, grad_keys, grad_values = tile_grads(
        query, grad_attn, row_lse, row_delta, own_qpos, group_keys, group_values, own_kpos
    )

    def pass_key_grads(key_grads):
        return passed_along((key_grads[0], key_grads[1]), "ctx", 1)

    def backward_hop(hop_index, loop_carry):
        query_sum, key_grads, cycle_keys, cycle_values = loop_carry
        cycle_keys, cycle_values = passed_along((cycle_keys, cycle_values), "ctx", 1)
        key_grads = pass_key_grads(key_grads)
        source = (ctx_index - hop_index) % ctx_size
        step_query, step_keys, step_values = tile_grads(
            query,
            grad_attn,
            row_lse,
            row_delta,
            own_qpos,
            cycle_keys,
            cycle_values,
            key_positions(source),
        )
        return (
            query_sum + step_query,
            (key_grads[0] + step_keys, key_grads[1] + step_values),
            cycle_keys,
            cycle_values,
        )

    result = lax.fori_loop(
        1, ctx_size, backward_hop, (grad_query, (grad_keys, grad_values), group_keys, group_values)
    )
    grad_query = result[0]
    key_grads = pass_key_grads(result[1])
    own_key_grad, own_value_grad = (
        lax.psum_scatter(key_grads[0], "fsdp", scatter_dimension=0, tiled=True),
        lax.psum_scatter(key_grads[1], "fsdp", scatter_dimension=0, tiled=True),
    )
    grad_query_rows = grad_query.reshape(rows, width)
    query_bias_grad = jnp.sum(grad_query_rows, axis=0)
    value_bias_grad = jnp.sum(own_value_grad, axis=0)
    grad_qkv = jnp.concatenate([grad_query_rows, own_key_grad, own_value_grad], axis=1).astype(
        jnp.bfloat16
    )
    qkv_weight_grad = rows_product(norm1, grad_qkv)
    grad_norm1 = transposed_product(grad_qkv, qkv_full)
    norm1_gain_grad = jnp.sum(grad_norm1 * normed1, axis=0)
    norm1_bias_grad = jnp.sum(grad_norm1, axis=0)
    input_grad = grad_middle + norm_backward(grad_norm1, gain_one, normed1, inv_std1)
    attn_shares = (
        lax.psum_scatter(norm1_gain_grad, "fsdp", scatter_dimension=0, tiled=True),
        lax.psum_scatter(norm1_bias_grad, "fsdp", scatter_dimension=0, tiled=True),
        lax.psum_scatter(qkv_weight_grad, "fsdp", scatter_dimension=0, tiled=True),
        lax.psum_scatter(query_bias_grad, "fsdp", scatter_dimension=0, tiled=True),
        lax.psum_scatter(value_bias_grad, "fsdp", scatter_dimension=0, tiled=True),
        lax.psum_scatter(proj_weight_grad, "fsdp", scatter_dimension=0, tiled=True),
        lax.psum_scatter(proj_bias_grad, "fsdp", scatter_dimension=0, tiled=True),
    )
    totals = lax.psum(
        (
            attn_shares[0],
            attn_shares[1],
            attn_shares[2],
            attn_shares[3],
            attn_shares[4],
            attn_shares[5],
            attn_shares[6],
            mlp_shares[0],
            mlp_shares[1],
            mlp_shares[2],
            mlp_shares[3],
            mlp_shares[4],
            mlp_shares[5],
        ),
        "ctx",
    )
    return (
        block_output,
        input_grad,
        totals[0],
        totals[1],
        totals[2],
        totals[3],
        totals[4],
        totals[5],
        totals[6],
        totals[7],
        totals[8],
        totals[9],
        totals[10],
        totals[11],
        totals[12],
    )


def head_cols(head, offset=0):
    return slice(offset + head * HEAD, offset + (head + 1) * HEAD)


def tile_keep(block, key_block, query_block):
    key_row = lax.broadcasted_iota(jnp.int32, (block, block), 0)
    query_col = lax.broadcasted_iota(jnp.int32, (block, block), 1)
    return key_row <= query_col + jnp.where(key_block == query_block, 0, block)


def forward_kernel(
    heads, block, ids_ref, own_ref, q_ref, kv_ref, out_ref, lse_ref, max_ref, sum_ref, acc_ref
):
    span = heads * HEAD
    max_ref[...] = jnp.full_like(max_ref, NEG_FILL)
    sum_ref[...] = jnp.zeros_like(sum_ref)
    acc_ref[...] = jnp.zeros_like(acc_ref)

    def step(index, carry):
        first = pl.multiple_of(index * block, block)
        key_block = ids_ref[index]
        for part in range(2):
            cols = slice(part * block, (part + 1) * block)
            query_block = own_ref[part]

            @pl.when(key_block <= query_block)
            def _():
                keep = tile_keep(block, key_block, query_block)
                for head in range(heads):
                    k = kv_ref[pl.ds(first, block), head_cols(head)]
                    v = kv_ref[pl.ds(first, block), head_cols(head, span)]
                    q = q_ref[cols, head_cols(head)]
                    scores = jnp.where(keep, transposed_product(k, q), NEG_FILL)
                    old_max = max_ref[head : head + 1, cols]
                    new_max = jnp.maximum(old_max, jnp.max(scores, axis=0, keepdims=True))
                    weights = jnp.exp(scores - new_max)
                    factor = jnp.exp(old_max - new_max)
                    max_ref[head : head + 1, cols] = new_max
                    sum_ref[head : head + 1, cols] = sum_ref[
                        head : head + 1, cols
                    ] * factor + jnp.sum(weights, axis=0, keepdims=True)
                    acc_ref[head_cols(head), cols] = acc_ref[
                        head_cols(head), cols
                    ] * factor + rows_product(v, weights.astype(jnp.bfloat16))

        return carry

    lax.fori_loop(0, kv_ref.shape[0] // block, step, 0)
    for head in range(heads):
        total = sum_ref[head : head + 1, :]
        out_ref[head_cols(head), :] = (acc_ref[head_cols(head), :] / total).astype(out_ref.dtype)
        lse_ref[head : head + 1, :] = max_ref[head : head + 1, :] + jnp.log(total)


def backward_kernel(
    heads, block, ids_ref, own_ref, q_ref, kv_ref, do_ref, lse_ref, delta_ref, dq_ref, dkv_ref, acc_ref
):
    span = heads * HEAD
    dq_ref[...] = jnp.zeros_like(dq_ref)

    def step(index, carry):
        first = pl.multiple_of(index * block, block)
        key_block = ids_ref[index]
        acc_ref[...] = jnp.zeros_like(acc_ref)
        for part in range(2):
            cols = slice(part * block, (part + 1) * block)
            query_block = own_ref[part]

            @pl.when(key_block <= query_block)
            def _():
                keep = tile_keep(block, key_block, query_block)
                key_parts = []
                value_parts = []
                for head in range(heads):
                    k = kv_ref[pl.ds(first, block), head_cols(head)]
                    v = kv_ref[pl.ds(first, block), head_cols(head, span)]
                    q = q_ref[cols, head_cols(head)]
                    do = do_ref[cols, head_cols(head)]
                    scores = jnp.where(keep, transposed_product(k, q), NEG_FILL)
                    probs = jnp.exp(scores - lse_ref[head : head + 1, cols])
                    value_parts.append(
                        jnp.dot(
                            probs.astype(jnp.bfloat16), do, preferred_element_type=jnp.float32
                        )
                    )
                    grad_probs = transposed_product(v, do)
                    grad_scores = (
                        probs * (grad_probs - delta_ref[head : head + 1, cols])
                    ).astype(jnp.bfloat16)
                    key_parts.append(
                        jnp.dot(grad_scores, q, preferred_element_type=jnp.float32)
                    )
                    dq_ref[head_cols(head), cols] += rows_product(k, grad_scores)
                acc_ref[...] += jnp.concatenate(key_parts + value_parts, axis=1)

        dkv_ref[pl.ds(first, block), :] = acc_ref[...].astype(dkv_ref.dtype)
        return carry

    lax.fori_loop(0, kv_ref.shape[0] // block, step, 0)


SMEM = pltpu.SMEM
VMEM = pltpu.VMEM


def attention_forward(heads, block, ids, own, q, kv):
    group_rows, span = q.shape
    return pl.pallas_call(
        functools.partial(forward_kernel, heads, block),
        out_shape=(
            jax.ShapeDtypeStruct((span, group_rows), jnp.bfloat16),
            jax.ShapeDtypeStruct((heads, group_rows), jnp.float32),
        ),
        in_specs=[pl.BlockSpec(memory_space=SMEM)] * 2 + [pl.BlockSpec(memory_space=VMEM)] * 2,
        out_specs=(pl.BlockSpec(memory_space=VMEM),) * 2,
        scratch_shapes=[
            VMEM((heads, group_rows), jnp.float32),
            VMEM((heads, group_rows), jnp.float32),
            VMEM((span, group_rows), jnp.float32),
        ],
        cost_estimate=pl.CostEstimate(
            flops=2 * group_rows * kv.shape[0] * span,
            bytes_accessed=2 * kv.size,
            transcendentals=group_rows * kv.shape[0] * heads // 2,
        ),
        name="attention_forward",
    )(ids, own, q, kv)


def attention_backward(heads, block, ids, own, q, kv, do, lse, delta):
    group_rows, span = q.shape
    return pl.pallas_call(
        functools.partial(backward_kernel, heads, block),
        out_shape=(
            jax.ShapeDtypeStruct((span, group_rows), jnp.float32),
            jax.ShapeDtypeStruct(kv.shape, jnp.bfloat16),
        ),
        in_specs=[pl.BlockSpec(memory_space=SMEM)] * 2 + [pl.BlockSpec(memory_space=VMEM)] * 5,
        out_specs=(pl.BlockSpec(memory_space=VMEM),) * 2,
        scratch_shapes=[VMEM((block, 2 * span), jnp.float32)],
        cost_estimate=pl.CostEstimate(
            flops=5 * group_rows * kv.shape[0] * span,
            bytes_accessed=4 * kv.size,
            transcendentals=group_rows * kv.shape[0] * heads // 2,
        ),
        name="attention_backward",
    )(ids, own, q, kv, do, lse, delta)


def head_shards(
    block_input,
    positions,
    norm1_gain,
    norm1_bias,
    qkv_weight,
    query_bias,
    value_bias,
    proj_weight,
    proj_bias,
    norm2_gain,
    norm2_bias,
    fc_weight,
    fc_bias,
    out_weight,
    out_bias,
    cotangent,
):
    rows, width = block_input.shape
    ctx_size = lax.axis_size("ctx")
    members = lax.axis_size("fsdp")
    ctx_index = lax.axis_index("ctx")
    member = lax.axis_index("fsdp")
    group_rows = rows * members
    block = group_rows // 2
    span = width // members
    heads = HEADS // members
    hidden = fc_weight.shape[1] // members
    piece = span // ctx_size
    f32, b16 = jnp.float32, jnp.bfloat16

    def gathered(value, axis=0):
        return lax.all_gather(value, "fsdp", axis=axis, tiled=True)

    def scattered(value):
        shares_in = lax.all_to_all(value.reshape(members, rows, width), "fsdp", 0, 0, tiled=True)
        return jnp.sum(shares_in.astype(f32), axis=0)

    def group_sum(value):
        return lax.psum_scatter(value, "ctx", scatter_dimension=0, tiled=True)[0]

    def exchanged(value):
        return lax.all_to_all(value, "fsdp", 0, 0, tiled=True)

    def own_rows(value):
        return lax.dynamic_slice_in_dim(value, member * rows, rows)

    vectors = jnp.concatenate(
        [norm1_gain, norm1_bias, proj_bias, norm2_gain, norm2_bias, out_bias]
    )
    vectors = jnp.pad(vectors, (0, 16 * width - vectors.size)).reshape(16, width)
    combined = lax.all_gather(
        jnp.concatenate([block_input, cotangent, vectors], axis=0), "fsdp", axis=0
    )
    input_all = combined[:, :rows].reshape(group_rows, width)
    cotangent_all = combined[:, rows : 2 * rows].reshape(group_rows, width)
    vectors = combined[:, 2 * rows :].reshape(members, 16 * width)[:, : 6 * span]
    vectors = vectors.reshape(members, 6, span).transpose(1, 0, 2).reshape(6, width)
    qkv_cols = exchanged(
        qkv_weight.reshape(span, 3, members, span).transpose(2, 0, 1, 3).reshape(members, span, 3 * span)
    ).reshape(width, 3 * span)
    gain_one, shift_one, pbias, gain_two, shift_two, obias = (vectors[i] for i in range(6))
    fc_cols = exchanged(fc_weight.reshape(span, members, hidden).transpose(1, 0, 2)).reshape(
        width, hidden
    )

    ids = positions.reshape(2 * ctx_size, block)[:, 0] // block
    own_ids = lax.dynamic_slice_in_dim(ids, 2 * ctx_index, 2)

    residual = input_all.astype(f32)
    norm1 = layer_norm(residual, gain_one, shift_one)[0].astype(b16)
    qkv = jnp.dot(norm1, qkv_cols, preferred_element_type=f32)
    query = (qkv[:, :span] + query_bias.astype(f32)).astype(b16)
    keys = qkv[:, span : 2 * span].astype(b16)
    values = (qkv[:, 2 * span :] + value_bias.astype(f32)).astype(b16)
    query = query * jnp.asarray(HEAD**-0.5, b16)
    all_kv = lax.all_gather(jnp.concatenate([keys, values], axis=1), "ctx", axis=0, tiled=True)
    all_kv, proj_late = lax.optimization_barrier((all_kv, proj_weight))
    proj_full = gathered(proj_late)
    attn_t, lse = attention_forward(heads, block, ids, own_ids, query, all_kv)
    attn_all_t = gathered(attn_t)
    middle_all = residual + rows_product(attn_all_t, proj_full) + pbias.astype(f32)
    norm2 = layer_norm(middle_all, gain_two, shift_two)[0].astype(b16)
    pre_act = jnp.dot(norm2, fc_cols, preferred_element_type=f32) + fc_bias.astype(f32)
    act = gelu_forward(pre_act).astype(b16)
    grad_act = transposed_product(cotangent_all, out_weight)
    grad_pre = grad_act * gelu_slope(pre_act)
    fc_bias_grad = jnp.sum(grad_pre, axis=0)
    grad_pre_half = grad_pre.astype(b16)
    grad_norm2 = scattered(transposed_product(grad_pre_half, fc_cols).astype(b16)).astype(f32)
    middle = own_rows(middle_all)
    _, normed2, inv_std2 = layer_norm(middle, gain_two, shift_two)
    grad_out = cotangent.astype(f32)
    grad_middle = grad_out + norm_backward(grad_norm2, gain_two, normed2, inv_std2)
    grad_middle_all = gathered(grad_middle.astype(b16))

    grad_attn = transposed_product(grad_middle_all, proj_weight).astype(b16)
    out_weight_grad = rows_product(act, cotangent_all).astype(b16)
    fc_weight_grad = rows_product(norm2, grad_pre_half).astype(b16)
    proj_weight_grad = jnp.dot(attn_t, grad_middle_all, preferred_element_type=f32).astype(b16)
    shares = jnp.concatenate(
        [
            out_weight_grad.reshape(ctx_size, -1, width),
            proj_weight_grad.reshape(ctx_size, piece, width),
            fc_weight_grad.reshape(members, ctx_size, piece, hidden)
            .transpose(1, 0, 2, 3)
            .reshape(ctx_size, members * piece, hidden),
        ],
        axis=1,
    )
    mlp_share = jnp.dot(act, out_weight, preferred_element_type=f32).astype(b16)
    grad_attn, shares, mlp_share = lax.optimization_barrier((grad_attn, shares, mlp_share))
    delta = jnp.sum(
        (grad_attn.T.astype(f32) * attn_t.astype(f32)).reshape(heads, HEAD, group_rows), axis=1
    )
    grad_query_t, grad_kv = attention_backward(
        heads, block, ids, own_ids, query, all_kv, grad_attn, lse, delta
    )
    block_output = middle + scattered(mlp_share).astype(f32) + obias.astype(f32)
    own_kv = group_sum(grad_kv.reshape(ctx_size, group_rows, 2 * span))

    shares = group_sum(shares)
    kept = shares.shape[0] - members * piece
    shares = jnp.concatenate([shares[:kept], exchanged(shares[kept:])], axis=0)
    shares = lax.all_gather(shares, "ctx", axis=0, tiled=False)
    out_rows = out_weight.shape[0] // ctx_size
    out_weight_grad = shares[:, :out_rows].reshape(out_weight.shape).astype(f32)
    proj_weight_grad = shares[:, out_rows:kept].reshape(proj_weight.shape).astype(f32)
    fc_weight_grad = (
        shares[:, kept:]
        .reshape(ctx_size, members, piece, hidden)
        .transpose(0, 2, 1, 3)
        .reshape(fc_weight.shape)
        .astype(f32)
    )

    grad_query = grad_query_t.T * HEAD**-0.5
    grad_qkv = jnp.concatenate([grad_query.astype(b16), own_kv], axis=1)
    grad_norm1 = scattered(transposed_product(grad_qkv, qkv_cols).astype(b16)).astype(f32)
    qkv_share = rows_product(norm1, grad_qkv).astype(b16)
    _, normed1, inv_std1 = layer_norm(block_input.astype(f32), gain_one, shift_one)
    input_grad = grad_middle + norm_backward(grad_norm1, gain_one, normed1, inv_std1)

    def pieces(vector):
        return vector.reshape(members, ctx_size, -1)

    def slotted(vector):
        own_slot = (jnp.arange(members) == member)[:, None, None]
        return jnp.where(own_slot, vector.reshape(1, ctx_size, -1), 0.0)

    riders = jnp.concatenate(
        [
            pieces(jnp.sum(grad_norm1 * normed1, axis=0)),
            pieces(jnp.sum(grad_norm1, axis=0)),
            pieces(jnp.sum(grad_middle, axis=0)),
            pieces(jnp.sum(grad_norm2 * normed2, axis=0)),
            pieces(jnp.sum(grad_norm2, axis=0)),
            pieces(jnp.sum(grad_out, axis=0)),
            slotted(jnp.sum(grad_query, axis=0)),
            slotted(jnp.sum(own_kv[:, span:].astype(f32), axis=0)),
            slotted(fc_bias_grad),
        ],
        axis=2,
    )
    used = riders.shape[2]
    riders = jnp.pad(riders, ((0, 0), (0, 0), (0, 3 * span - used))).astype(b16)
    qkv_share = jnp.concatenate(
        [
            qkv_share.reshape(members, ctx_size, piece, 3 * span),
            jnp.broadcast_to(riders[:, :, None], (members, ctx_size, 8, 3 * span)),
        ],
        axis=2,
    )
    deep = piece + 8
    qkv_share = qkv_share.transpose(1, 0, 2, 3).reshape(ctx_size, members * deep, 3 * span)
    qkv_share = group_sum(qkv_share)
    qkv_share = lax.all_gather(exchanged(qkv_share), "ctx", axis=0, tiled=False)
    qkv_share = qkv_share.reshape(ctx_size, members, deep, 3 * span)
    qkv_weight_grad = (
        qkv_share[:, :, :piece]
        .reshape(ctx_size, members, piece, 3, span)
        .transpose(0, 2, 3, 1, 4)
        .reshape(qkv_weight.shape)
        .astype(f32)
    )
    sums = jnp.sum(qkv_share[:, :, piece, :used].astype(f32), axis=1)
    parts = [sums[:, i * piece : (i + 1) * piece].reshape(span) for i in range(8)]
    return (
        block_output,
        input_grad,
        parts[0],
        parts[1],
        qkv_weight_grad,
        parts[6],
        parts[7],
        proj_weight_grad,
        parts[2],
        parts[3],
        parts[4],
        fc_weight_grad,
        sums[:, 8 * piece :].reshape(hidden),
        out_weight_grad,
        parts[5],
    )


def solution(mesh):
    in_specs = (
        P(("ctx", "fsdp"), None),
        P(),
        P("fsdp"),
        P("fsdp"),
        P("fsdp", None),
        P("fsdp"),
        P("fsdp"),
        P("fsdp", None),
        P("fsdp"),
        P("fsdp"),
        P("fsdp"),
        P("fsdp", None),
        P("fsdp"),
        P("fsdp", None),
        P("fsdp"),
        P(("ctx", "fsdp"), None),
    )
    out_specs = (
        P(("ctx", "fsdp"), None),
        P(("ctx", "fsdp"), None),
        P("fsdp"),
        P("fsdp"),
        P("fsdp", None),
        P("fsdp"),
        P("fsdp"),
        P("fsdp", None),
        P("fsdp"),
        P("fsdp"),
        P("fsdp"),
        P("fsdp", None),
        P("fsdp"),
        P("fsdp", None),
        P("fsdp"),
    )
    members = mesh.shape["fsdp"]
    by_heads = HEADS % members == 0 and (HEADS // members * HEAD) % mesh.shape["ctx"] == 0
    body = head_shards if by_heads else shards
    return jax.shard_map(body, mesh=mesh, in_specs=in_specs, out_specs=out_specs, check_vma=False)
```
